512 devices in a mesh: dp: 16 (over z_lo, core), tensor: 32 (over x, z_hi, y).
Axes of the slice: x: 4, y: 4, z: 16 (z_hi: 2, z_lo: 8; z = z_hi * 8 + z_lo), core: 2. Of those that a mesh axis runs over, the one named last changes fastest.
Arguments:
- activations: bfloat16 [8192, 8192], P('dp', 'tensor'), may hold values from -6 to 6
- left_factor: bfloat16 [1024, 8192], P(None, 'tensor'), may hold values from -0.0625 to 0.0625
- right_factor: bfloat16 [1024, 16384], P(None, 'tensor'), may hold values from -0.1875 to 0.1875
- out_grad: bfloat16 [8192, 16384], P('dp', 'tensor'), may hold values from -6 to 6
Outputs:
- input_grad: bfloat16 [8192, 8192], P('dp', 'tensor')
- left_grad: float32 [1024, 8192], P('dp', 'tensor')
- right_grad: float32 [1024, 16384], P('dp', 'tensor')
The draws below stay inside these ranges and needn't reach their ends.
All inputs are finite; a program needn't handle non-finite values.
Results may differ from the reference program's by a relative error of at most 0.0049.
Values may be sent and summed in bfloat16 or wider, within the bound.
A program may use at most 64 MiB of HBM per device.

```python
import math
import jax
import jax.numpy as jnp
from jax import lax

D = 8192
FF = 16384
R = 1024
TOKENS = 8192


def levels(rng, extent, pieces, smallest, largest):
    def one(axis_at, shards_of):
        heights = jax.random.uniform(jax.random.fold_in(jax.random.fold_in(rng, 6), axis_at), (shards_of,), jnp.float32, smallest / len(pieces), largest / len(pieces))
        return jnp.repeat(jnp.exp(heights), extent[axis_at] // shards_of).reshape((-1,) + (1,) * (len(extent) - axis_at - 1))

    loudness = one(*pieces[0])
    for cut in pieces[1:]:
        loudness = loudness * one(*cut)
    return loudness


def bell_draw(own_key, shape, deviation, bound, split=(), dtype=jnp.bfloat16):
    level = levels(own_key, shape, split, -0.22, 0.18) if split else 1.0
    entries = jax.random.normal(own_key, shape, jnp.float32) * deviation * level
    return jnp.minimum(jnp.maximum(entries, -bound), bound).astype(dtype)


def setup_inputs(seed: int = 0) -> dict:
    key_of = jax.random.split(jax.random.key(seed), 5)
    return {
        "activations": bell_draw(key_of[0], (TOKENS, D), 1.0, 6.0, ((0, 16), (1, 32))),
        "left_factor": bell_draw(key_of[1], (R, D), D ** -0.5, 0.0625, ((1, 32),)),
        "right_factor": bell_draw(key_of[2], (R, FF), R ** -0.5, 0.1875, ((1, 32),)),
        "out_grad": bell_draw(key_of[3], (TOKENS, FF), 1.0, 6.0, ((0, 16), (1, 32))),
    }


def reference(activations, left_factor, right_factor, out_grad):
    dims = (((1,), (1,)), ((), ()))
    latent = lax.dot_general(activations, left_factor, dims, preferred_element_type=jnp.float32).astype(jnp.bfloat16)
    latent_grad = lax.dot_general(out_grad, right_factor, dims, preferred_element_type=jnp.float32).astype(jnp.bfloat16)
    input_grad = jnp.dot(latent_grad, left_factor, preferred_element_type=jnp.float32).astype(jnp.bfloat16)
    scale = 1.0 / math.sqrt(TOKENS)
    rows = (((0,), (0,)), ((), ()))
    right_grad = lax.dot_general(latent, out_grad, rows, preferred_element_type=jnp.float32) * scale
    left_grad = lax.dot_general(latent_grad, activations, rows, preferred_element_type=jnp.float32) * scale
    return (input_grad, left_grad, right_grad)
```

```python
import functools
import math

import jax
import jax.numpy as jnp
from jax import lax
from jax.experimental import pallas as pl
from jax.experimental.pallas import tpu as pltpu
from jax.sharding import PartitionSpec as P

MESH = pl.DeviceIdType.MESH
F32, BF16 = jnp.float32, jnp.bfloat16
NT = (((1,), (1,)), ((), ()))
TN = (((0,), (0,)), ((), ()))


def place(x, y, z, core):
    x, y, z, core = x % 4, y % 4, z % 16, core % 2
    return ((z % 8) * 2 + core, x * 8 + (z // 8) * 4 + y)


def kernel(
    scale,
    act_hbm, left_hbm, right_hbm, cot_hbm,
    ig_ref, lg_ref, rg_ref,
    act, left, right, cot,
    own1, snd1, rcv1, acc2, snd2, rcv2, acc3, snd3, rcv3, lat,
    cs_r, cr_r, cs_l, cr_l, ps_r, pr_r, ps_l, pr_l, ds_r, dr_r, ds_l, dr_l, sum_r, sum_l, fin_r, fin_l,
    in_sem, s1, r1, s2, r2, s3, r3, s4, r4, s5, r5, sc, rc, sp, rp, sd, rd,
):
    d, t = lax.axis_index("dp"), lax.axis_index("tensor")
    x, y, core = t // 8, t % 4, d % 2
    zl = d // 2
    z = ((t // 4) % 2) * 8 + zl
    parity, mine = zl % 2, zl // 2

    def coords(h):
        return (x, y) if h == 0 else (y, x)

    def along(h, da, db):
        return place(x + da, y + db, z, core) if h == 0 else place(x + db, y + da, z, core)

    def remote(src, dst, ssem, rsem, device):
        return pltpu.make_async_remote_copy(
            src_ref=src, dst_ref=dst, send_sem=ssem, recv_sem=rsem,
            device_id=device, device_id_type=MESH,
        )

    loads = [
        pltpu.make_async_copy(src, dst, in_sem.at[i])
        for i, (src, dst) in enumerate(
            ((left_hbm, left), (act_hbm, act), (right_hbm, right), (cot_hbm, cot))
        )
    ]
    for load in loads:
        load.start()

    barrier = pltpu.get_barrier_semaphore()
    peers = [place(x, y, z + 8, core)]
    peers += [place(x, y, (z // 8) * 8 + ((mine + k) % 4) * 2 + parity, core) for k in (2, 1, 3)]
    peers += [place(x, y, (z // 8) * 8 + mine * 2 + 1 - parity, core)]
    peers += [place(x + k, y, z, core) for k in (2, 1, 3)] + [place(x, y + k, z, core) for k in (2, 1, 3)]
    peers += [place(x, y, z, core + 1)]
    for peer in peers:
        pl.semaphore_signal(barrier, inc=1, device_id=peer, device_id_type=MESH)

    def copy1(k, step):
        a, _ = coords(k % 2)
        return remote(
            snd1.at[k, step - 1], rcv1.at[k, step - 1], s1.at[k, step - 1], r1.at[k, step - 1],
            along(k % 2, step, 0),
        )

    def partial_tile(k, step, weights, feats):
        h = k % 2
        a, _ = coords(h)
        row = pl.multiple_of(h * 512 + ((a + step) % 4) * 128, 128)
        tile = lax.dot_general(weights[pl.ds(row, 128), :], feats[...], NT, preferred_element_type=F32)
        tile = tile.reshape(4, 32, 512)
        if step:
            snd1[k, step - 1] = tile.astype(BF16)
        else:
            own1[k] = tile

    order = [(h, step) for step in (2, 1, 3) for h in (0, 1)]
    loads[0].wait()
    loads[1].wait()
    waiting = None
    for n, (h, step) in enumerate(order):
        partial_tile(h, step, left, act)
        if n == 0:
            pl.semaphore_wait(barrier, len(peers))
        if waiting:
            copy1(*waiting).start()
        waiting = (h, step)
    partial_tile(0, 0, left, act)
    copy1(*waiting).start()
    partial_tile(1, 0, left, act)
    loads[2].wait()
    loads[3].wait()
    waiting = None
    for h, step in order:
        partial_tile(2 + h, step, right, cot)
        if waiting:
            copy1(*waiting).start()
        waiting = (2 + h, step)
    partial_tile(2, 0, right, cot)
    copy1(*waiting).start()
    partial_tile(3, 0, right, cot)

    def copy2(k, step):
        _, b = coords(k % 2)
        return remote(
            snd2.at[k, (b + step) % 4], rcv2.at[k, step - 1], s2.at[k, step - 1], r2.at[k, step - 1],
            along(k % 2, 0, step),
        )

    def second(k):
        for step in (1, 3, 2):
            copy1(k, step).wait_recv()
        total = own1[k] + rcv1[k, 0].astype(F32) + rcv1[k, 1].astype(F32) + rcv1[k, 2].astype(F32)
        acc2[k] = total
        snd2[k] = total.astype(BF16)
        for step in (2, 1, 3):
            copy2(k, step).start()

    def copy3(k):
        return remote(snd3.at[k], rcv3.at[k], s3.at[k], r3.at[k], place(x, y, z + 8, core))

    def third(k):
        _, b = coords(k % 2)
        for step in (1, 3, 2):
            copy2(k, step).wait_recv()
        total = acc2[k, b] + rcv2[k, 0].astype(F32) + rcv2[k, 1].astype(F32) + rcv2[k, 2].astype(F32)
        acc3[k] = total
        snd3[k] = total.astype(BF16)
        copy3(k).start()

    def copy4(k, step, arriving=False):
        a, b = coords(k % 2)
        block = lat.at[k, a, (b - step) % 4] if arriving else lat.at[k, a, b]
        return remote(block, block, s4.at[k, step - 1], r4.at[k, step - 1], along(k % 2, 0, step))

    def copy5(k, back, step, arriving=False):
        a, b = coords(k % 2)
        block = lat.at[k, (a - step) % 4 if arriving else a, (b - back) % 4]
        return remote(
            block, block, s5.at[k, back, step - 1], r5.at[k, back, step - 1], along(k % 2, step, 0)
        )

    def fourth(k):
        a, b = coords(k % 2)
        copy3(k).wait_recv()
        lat[k, a, b] = (acc3[k] + rcv3[k].astype(F32)).astype(BF16)
        for step in (2, 1, 3):
            copy4(k, step).start()
        for step in (2, 1, 3):
            copy5(k, 0, step).start()

    def fifth(k):
        for back in (1, 3, 2):
            copy4(k, back, True).wait_recv()
            for step in (2, 1, 3):
                copy5(k, back, step).start()

    def gathered(k):
        for back in (0, 1, 3, 2):
            for step in (1, 3, 2):
                copy5(k, back, step, True).wait_recv()

    for k in range(4):
        second(k)
    for k in range(4):
        third(k)
    for k in range(4):
        fourth(k)
        if k >= 2:
            fifth(k - 2)
    for k in (2, 3):
        fifth(k)

    def sets(k):
        if k < 2:
            return cot, cs_r, cr_r, ps_r, pr_r, sum_r
        return act, cs_l, cr_l, ps_l, pr_l, sum_l

    def core_copy(k):
        _, cs, cr, _, _, _ = sets(k)
        return remote(cs.at[k % 2], cr.at[k % 2], sc.at[k], rc.at[k], place(x, y, z, core + 1))

    def products(k):
        feats, cs, _, _, _, total = sets(k)
        width = feats.shape[1]
        theirs = lat[k, :, pl.ds(2 - 2 * core, 2)].reshape(256, 512)
        cs[k % 2] = jnp.dot(theirs, feats[...], preferred_element_type=F32).reshape(4, 64, width).astype(BF16)
        ours = lat[k, :, pl.ds(2 * core, 2)].reshape(256, 512)
        result = jnp.dot(ours, feats[...], preferred_element_type=F32).reshape(4, 64, width)
        core_copy(k).start()
        total[k % 2] = result

    def pair_copy(k):
        _, _, _, ps, pr, _ = sets(k)
        return remote(
            ps.at[k % 2], pr.at[k % 2], sp.at[k], rp.at[k],
            place(x, y, (z // 8) * 8 + mine * 2 + 1 - parity, core),
        )

    def paired(k):
        _, _, cr, ps, _, total = sets(k)
        core_copy(k).wait_recv()
        for j in range(2):
            other = 2 * j + 1 - parity
            ps[k % 2, j] = (total[k % 2, other] + cr[k % 2, other].astype(F32)).astype(BF16)
        pair_copy(k).start()

    def direct_copy(kind, m):
        ds, dr = (ds_r, dr_r) if kind == 0 else (ds_l, dr_l)
        slot = (m - mine + 3) % 4
        return remote(
            ds.at[m], dr.at[slot], sd.at[kind, m], rd.at[kind, slot],
            place(x, y, (z // 8) * 8 + m * 2 + parity, core),
        )

    def direct(k):
        _, _, cr, _, pr, total = sets(k)
        kind = k // 2
        ds, fin = (ds_r, fin_r) if kind == 0 else (ds_l, fin_l)
        pair_copy(k).wait_recv()
        for j in range(2):
            m = (k % 2) * 2 + j
            ours = 2 * j + parity
            value = total[k % 2, ours] + cr[k % 2, ours].astype(F32) + pr[k % 2, j].astype(F32)

            @pl.when(m != mine)
            def _():
                ds[m] = value.astype(BF16)
                direct_copy(kind, m).start()

            @pl.when(m == mine)
            def _():
                fin[...] = value

    def arrived(kind):
        dr, fin, out = (dr_r, fin_r, rg_ref) if kind == 0 else (dr_l, fin_l, lg_ref)
        total = fin[...]
        for slot in (0, 2, 1):
            remote(
                dr.at[slot], dr.at[slot], sd.at[kind, slot], rd.at[kind, slot], place(x, y, z + 8, core)
            ).wait_recv()
            total = total + dr[slot].astype(F32)
        out[...] = total * scale

    for k in (0, 1):
        gathered(k)
        products(k)
    for k in (0, 1):
        paired(k)
    for k in (0, 1):
        direct(k)
    for k in (2, 3):
        gathered(k)
        products(k)
    for k in (2, 3):
        paired(k)
    for k in (2, 3):
        direct(k)

    for n in range(2):
        rows = pl.ds(n * 256, 256)
        total = lax.dot_general(
            lat[2, :, :, :, rows].reshape(512, 256), left[0:512, :], TN, preferred_element_type=F32
        )
        total += lax.dot_general(
            lat[3, :, :, :, rows].reshape(512, 256), left[512:1024, :], TN, preferred_element_type=F32
        )
        ig_ref[rows, :] = total.astype(BF16)

    arrived(0)
    arrived(1)

    for k in range(4):
        for step in (1, 2, 3):
            copy1(k, step).wait_send()
            copy2(k, step).wait_send()
            copy4(k, step).wait_send()
            for back in range(4):
                copy5(k, back, step).wait_send()
        copy3(k).wait_send()
        core_copy(k).wait_send()
        pair_copy(k).wait_send()
    for kind in range(2):
        for m in range(4):
            @pl.when(m != mine)
            def _():
                direct_copy(kind, m).wait_send()


def shards(activations, left_factor, right_factor, out_grad):
    scale = 1.0 / math.sqrt(activations.shape[0] * lax.axis_size("dp"))
    hbm = pl.BlockSpec(memory_space=pl.ANY)
    vmem = pl.BlockSpec(memory_space=pltpu.VMEM)
    dma = pltpu.SemaphoreType.DMA
    return pl.pallas_call(
        functools.partial(kernel, scale),
        name="lowrank_backward",
        out_shape=(
            jax.ShapeDtypeStruct((512, 256), BF16),
            jax.ShapeDtypeStruct((64, 256), F32),
            jax.ShapeDtypeStruct((64, 512), F32),
        ),
        in_specs=[hbm] * 4,
        out_specs=(vmem,) * 3,
        scratch_shapes=[
            pltpu.VMEM((512, 256), BF16),
            pltpu.VMEM((1024, 256), BF16),
            pltpu.VMEM((1024, 512), BF16),
            pltpu.VMEM((512, 512), BF16),
            pltpu.VMEM((4, 4, 32, 512), F32),
            pltpu.VMEM((4, 3, 4, 32, 512), BF16),
            pltpu.VMEM((4, 3, 4, 32, 512), BF16),
            pltpu.VMEM((4, 4, 32, 512), F32),
            pltpu.VMEM((4, 4, 32, 512), BF16),
            pltpu.VMEM((4, 3, 32, 512), BF16),
            pltpu.VMEM((4, 32, 512), F32),
            pltpu.VMEM((4, 32, 512), BF16),
            pltpu.VMEM((4, 32, 512), BF16),
            pltpu.VMEM((4, 4, 4, 32, 512), BF16),
            pltpu.VMEM((2, 4, 64, 512), BF16),
            pltpu.VMEM((2, 4, 64, 512), BF16),
            pltpu.VMEM((2, 4, 64, 256), BF16),
            pltpu.VMEM((2, 4, 64, 256), BF16),
            pltpu.VMEM((2, 2, 64, 512), BF16),
            pltpu.VMEM((2, 2, 64, 512), BF16),
            pltpu.VMEM((2, 2, 64, 256), BF16),
            pltpu.VMEM((2, 2, 64, 256), BF16),
            pltpu.VMEM((4, 64, 512), BF16),
            pltpu.VMEM((3, 64, 512), BF16),
            pltpu.VMEM((4, 64, 256), BF16),
            pltpu.VMEM((3, 64, 256), BF16),
            pltpu.VMEM((2, 4, 64, 512), F32),
            pltpu.VMEM((2, 4, 64, 256), F32),
            pltpu.VMEM((64, 512), F32),
            pltpu.VMEM((64, 256), F32),
            dma((4,)),
            dma((4, 3)), dma((4, 3)),
            dma((4, 3)), dma((4, 3)),
            dma((4,)), dma((4,)),
            dma((4, 3)), dma((4, 3)),
            dma((4, 4, 3)), dma((4, 4, 3)),
            dma((4,)), dma((4,)),
            dma((4,)), dma((4,)),
            dma((2, 4)), dma((2, 3)),
        ],
        compiler_params=pltpu.CompilerParams(
            collective_id=0, has_side_effects=True, vmem_limit_bytes=48 * 1024 * 1024
        ),
    )(activations, left_factor, right_factor, out_grad)


def solution(mesh):
    return jax.shard_map(
        shards,
        mesh=mesh,
        in_specs=(P("dp", "tensor"), P(None, "tensor"), P(None, "tensor"), P("dp", "tensor")),
        out_specs=(P("dp", "tensor"),) * 3,
        check_vma=False,
    )
```

```python
import functools
import math

import jax
import jax.numpy as jnp
from jax import lax
from jax.experimental import pallas as pl
from jax.experimental.pallas import tpu as pltpu
from jax.sharding import PartitionSpec as P

MESH = pl.DeviceIdType.MESH
F32, BF16 = jnp.float32, jnp.bfloat16
NT = (((1,), (1,)), ((), ()))
TN = (((0,), (0,)), ((), ()))


def place(x, y, z, core):
    x, y, z, core = x % 4, y % 4, z % 16, core % 2
    return ((z % 8) * 2 + core, x * 8 + (z // 8) * 4 + y)


def kernel(
    scale,
    act_hbm, left_hbm, right_hbm, cot_hbm,
    ig_ref, lg_ref, rg_ref,
    act, left, right, cot,
    own1, snd1, rcv1, acc2, snd2, rcv2, acc3, snd3, rcv3, lat,
    latx, qs_r, qr_r, qs_l, qr_l, hs_r, hr_r, hs_l, hr_l, sum_r, sum_l,
    in_sem, s1, r1, s2, r2, s3, r3, s4, r4, s5, r5, sx, rx, sq, rq, sh, rh,
):
    d, t = lax.axis_index("dp"), lax.axis_index("tensor")
    x, y, core = t // 8, t % 4, d % 2
    zl = d // 2
    z = ((t // 4) % 2) * 8 + zl
    quad, pos = zl // 4, zl % 4

    def coords(h):
        return (x, y) if h == 0 else (y, x)

    def along(h, da, db):
        return place(x + da, y + db, z, core) if h == 0 else place(x + db, y + da, z, core)

    def remote(src, dst, ssem, rsem, device):
        return pltpu.make_async_remote_copy(
            src_ref=src, dst_ref=dst, send_sem=ssem, recv_sem=rsem,
            device_id=device, device_id_type=MESH,
        )

    def mate(step):
        return place(x, y, z - pos + (pos + step) % 4, core)

    opposite = place(x, y, z + 4 - 8 * quad, core)

    loads = [
        pltpu.make_async_copy(src, dst, in_sem.at[i])
        for i, (src, dst) in enumerate(
            ((left_hbm, left), (act_hbm, act.at[core]), (right_hbm, right), (cot_hbm, cot.at[core]))
        )
    ]
    for load in loads:
        load.start()

    barrier = pltpu.get_barrier_semaphore()
    peers = [place(x, y, z + 8, core), place(x, y, z + 8, core + 1)]
    peers += [opposite, *(mate(step) for step in (2, 1, 3))]
    peers += [place(x + k, y, z, core) for k in (2, 1, 3)] + [place(x, y + k, z, core) for k in (2, 1, 3)]
    peers += [place(x, y, z, core + 1)]
    for peer in peers:
        pl.semaphore_signal(barrier, inc=1, device_id=peer, device_id_type=MESH)

    def copy1(k, step):
        a, _ = coords(k % 2)
        return remote(
            snd1.at[k, step - 1], rcv1.at[k, step - 1], s1.at[k, step - 1], r1.at[k, step - 1],
            along(k % 2, step, 0),
        )

    def feature_copies():
        return [
            remote(src, dst.at[core], sx.at[i], rx.at[i], place(x, y, z, core + 1))
            for i, (src, dst) in enumerate(((cot_hbm, cot), (act_hbm, act)))
        ]

    def partial_tile(k, step, weights, feats):
        h = k % 2
        a, _ = coords(h)
        row = pl.multiple_of(h * 512 + ((a + step) % 4) * 128, 128)
        tile = lax.dot_general(weights[pl.ds(row, 128), :], feats[core], NT, preferred_element_type=F32)
        for c in range(2):
            rows = tile[c * 64 : c * 64 + 64].reshape(4, 16, 512)
            if step:
                snd1[k, step - 1, :, c] = rows.astype(BF16)
            else:
                own1[k, :, c] = rows

    order = [(h, step) for step in (2, 1, 3) for h in (0, 1)]
    loads[0].wait()
    loads[1].wait()
    waiting = None
    for n, (h, step) in enumerate(order):
        partial_tile(h, step, left, act)
        if n == 0:
            pl.semaphore_wait(barrier, len(peers))
        if waiting:
            copy1(*waiting).start()
        waiting = (h, step)
    partial_tile(0, 0, left, act)
    copy1(*waiting).start()
    for copy in feature_copies():
        copy.start()
    partial_tile(1, 0, left, act)
    loads[2].wait()
    loads[3].wait()
    for n, (h, step) in enumerate(order):
        partial_tile(2 + h, step, right, cot)
    partial_tile(2, 0, right, cot)
    partial_tile(3, 0, right, cot)

    def copy2(k, step):
        _, b = coords(k % 2)
        return remote(
            snd2.at[k, (b + step) % 4], rcv2.at[k, step - 1], s2.at[k, step - 1], r2.at[k, step - 1],
            along(k % 2, 0, step),
        )

    def second(k):
        for step in (1, 3, 2) if k >= 2 else (1, 3):
            copy1(k, step).wait_recv()
        total = own1[k] + rcv1[k, 0].astype(F32) + rcv1[k, 1].astype(F32) + rcv1[k, 2].astype(F32)
        acc2[k] = total
        snd2[k] = total.astype(BF16)
        for step in (2, 1, 3):
            copy2(k, step).start()

    def copy3(k, way):
        source = snd3.at[k, core if way == 0 else 1 - core]
        device = (place(x, y, z + 8, core), place(x, y, z, core + 1), place(x, y, z + 8, core + 1))[way]
        return remote(source, rcv3.at[k, way], s3.at[k, way], r3.at[k, way], device)

    def third(k):
        _, b = coords(k % 2)
        for step in (1, 3, 2):
            copy2(k, step).wait_recv()
        total = acc2[k, b] + rcv2[k, 0].astype(F32) + rcv2[k, 1].astype(F32) + rcv2[k, 2].astype(F32)
        acc3[k] = total
        snd3[k] = total.astype(BF16)
        for way in (0, 2, 1):
            copy3(k, way).start()

    def copy4(k, step, arriving=False):
        a, b = coords(k % 2)
        block = lat.at[k, a, (b - step) % 4] if arriving else lat.at[k, a, b]
        return remote(block, block, s4.at[k, step - 1], r4.at[k, step - 1], along(k % 2, 0, step))

    def copy5(k, back, step, arriving=False):
        a, b = coords(k % 2)
        block = lat.at[k, (a - step) % 4 if arriving else a, (b - back) % 4]
        return remote(
            block, block, s5.at[k, back, step - 1], r5.at[k, back, step - 1], along(k % 2, step, 0)
        )

    def fourth(k):
        a, b = coords(k % 2)
        for way in (1, 0, 2):
            copy3(k, way).wait_recv()
        lat[k, a, b, core] = (acc3[k, core] + rcv3[k, 0].astype(F32)).astype(BF16)
        lat[k, a, b, 1 - core] = (rcv3[k, 1].astype(F32) + rcv3[k, 2].astype(F32)).astype(BF16)
        for step in (2, 1, 3):
            copy4(k, step).start()
        for step in (2, 1, 3):
            copy5(k, 0, step).start()

    def fifth(k):
        for back in (1, 3, 2):
            copy4(k, back, True).wait_recv()
            for step in (2, 1, 3):
                copy5(k, back, step).start()

    def gathered(k):
        for back in (0, 1, 3, 2):
            for step in (1, 3, 2):
                copy5(k, back, step, True).wait_recv()

    for k in (0, 1):
        copy1(k, 2).wait_recv()
        copy1(2 + k, 2).start()
    for k in (0, 1):
        second(k)
    for h, step in order[2:]:
        copy1(2 + h, step).start()
    for k in (0, 1):
        third(k)
    for k in (2, 3):
        second(k)
    for k in (2, 3):
        third(k)
    for k in (0, 1):
        fourth(k)
    for k in (0, 1):
        fifth(k)
    for k in (2, 3):
        fourth(k)

    kinds = (
        (cot, qs_r, qr_r, hs_r, hr_r, sum_r, rg_ref),
        (act, qs_l, qr_l, hs_l, hr_l, sum_l, lg_ref),
    )

    def products(kind, part):
        feats, total = kinds[kind][0], kinds[kind][5]
        k = kind * 2 + (quad if part else 1 - quad)
        result = jnp.dot(lat[k, :, :, 0].reshape(256, 512), feats[0], preferred_element_type=F32)
        result += jnp.dot(lat[k, :, :, 1].reshape(256, 512), feats[1], preferred_element_type=F32)
        total[part] = result.reshape(4, 64, feats.shape[2])

    def swap_copy(h):
        return remote(
            lat.at[2 + h, :, :, 1 - core], latx.at[h], sx.at[2 + h], rx.at[2 + h], place(x, y, z, core + 1)
        )

    def quad_copy(kind, part, step):
        qs, qr = kinds[kind][1:3]
        return remote(
            qs.at[part, step - 1], qr.at[part, step - 1],
            sq.at[kind, part, step - 1], rq.at[kind, part, step - 1], mate(step),
        )

    def quads(kind, part):
        qs, total = kinds[kind][1], kinds[kind][5]
        for step in (2, 1, 3):
            qs[part, step - 1] = total[part, (pos + step) % 4].astype(BF16)
        for step in (2, 1, 3):
            quad_copy(kind, part, step).start()

    def run_sum(kind, part):
        qr = kinds[kind][2]
        total = kinds[kind][5][part, pos]
        for step in (1, 3, 2):
            quad_copy(kind, part, step).wait_recv()
            total = total + qr[part, step - 1].astype(F32)
        return total

    def half_copy(kind):
        hs, hr = kinds[kind][3:5]
        return remote(hs, hr, sh.at[kind], rh.at[kind], opposite)

    def halves(kind):
        hs = kinds[kind][3]
        hs[...] = run_sum(kind, 0).astype(BF16)
        half_copy(kind).start()

    def finish(kind):
        hr, out = kinds[kind][4], kinds[kind][6]
        total = run_sum(kind, 1)
        half_copy(kind).wait_recv()
        out[...] = (total + hr[...].astype(F32)) * scale

    for copy in feature_copies():
        copy.wait_recv()
    gathered(0)
    gathered(1)
    products(0, 0)
    quads(0, 0)
    fifth(2)
    fifth(3)
    products(0, 1)
    gathered(2)
    gathered(3)
    products(1, 0)
    quads(1, 0)
    halves(0)
    quads(0, 1)
    for h in range(2):
        swap_copy(h).start()
    products(1, 1)
    quads(1, 1)

    def ranks(h, c):
        return jnp.concatenate(
            [left[pl.ds(pl.multiple_of(h * 512 + i * 128 + c * 64, 64), 64), :] for i in range(4)], axis=0
        )

    for h in range(2):
        swap_copy(h).wait_recv()
    total = 0.0
    for h in range(2):
        total += lax.dot_general(
            lat[2 + h, :, :, core].reshape(256, 512), ranks(h, core), TN, preferred_element_type=F32
        )
        total += lax.dot_general(
            latx[h].reshape(256, 512), ranks(h, 1 - core), TN, preferred_element_type=F32
        )
    ig_ref[...] = total.astype(BF16)
    halves(1)
    finish(0)
    finish(1)

    for k in range(4):
        for step in (1, 2, 3):
            copy1(k, step).wait_send()
            copy2(k, step).wait_send()
            copy4(k, step).wait_send()
            for back in range(4):
                copy5(k, back, step).wait_send()
        for way in range(3):
            copy3(k, way).wait_send()
    for copy in feature_copies():
        copy.wait_send()
    for kind in range(2):
        swap_copy(kind).wait_send()
        half_copy(kind).wait_send()
        for part in range(2):
            for step in (1, 2, 3):
                quad_copy(kind, part, step).wait_send()


def put_out(a, b, c, a_out, b_out, c_out, sem):
    copies = [
        pltpu.make_async_copy(src, dst, sem.at[i])
        for i, (src, dst) in enumerate(((a, a_out), (b, b_out), (c, c_out)))
    ]
    for copy in copies:
        copy.start()
    for copy in copies:
        copy.wait()


def shards(activations, left_factor, right_factor, out_grad):
    scale = 1.0 / math.sqrt(activations.shape[0] * lax.axis_size("dp"))
    hbm = pl.BlockSpec(memory_space=pltpu.HBM)
    vmem = pl.BlockSpec(memory_space=pltpu.VMEM)
    dma = pltpu.SemaphoreType.DMA
    results = pl.pallas_call(
        functools.partial(kernel, scale),
        name="lowrank_backward",
        out_shape=(
            jax.ShapeDtypeStruct((512, 256), BF16),
            jax.ShapeDtypeStruct((64, 256), F32),
            jax.ShapeDtypeStruct((64, 512), F32),
        ),
        in_specs=[hbm] * 4,
        out_specs=(vmem,) * 3,
        scratch_shapes=[
            pltpu.VMEM((2, 512, 256), BF16),
            pltpu.VMEM((1024, 256), BF16),
            pltpu.VMEM((1024, 512), BF16),
            pltpu.VMEM((2, 512, 512), BF16),
            pltpu.VMEM((4, 4, 2, 16, 512), F32),
            pltpu.VMEM((4, 3, 4, 2, 16, 512), BF16),
            pltpu.VMEM((4, 3, 4, 2, 16, 512), BF16),
            pltpu.VMEM((4, 4, 2, 16, 512), F32),
            pltpu.VMEM((4, 4, 2, 16, 512), BF16),
            pltpu.VMEM((4, 3, 2, 16, 512), BF16),
            pltpu.VMEM((4, 2, 16, 512), F32),
            pltpu.VMEM((4, 2, 16, 512), BF16),
            pltpu.VMEM((4, 3, 16, 512), BF16),
            pltpu.VMEM((4, 4, 4, 2, 16, 512), BF16),
            pltpu.VMEM((2, 4, 4, 16, 512), BF16),
            pltpu.VMEM((2, 3, 64, 512), BF16),
            pltpu.VMEM((2, 3, 64, 512), BF16),
            pltpu.VMEM((2, 3, 64, 256), BF16),
            pltpu.VMEM((2, 3, 64, 256), BF16),
            pltpu.VMEM((64, 512), BF16),
            pltpu.VMEM((64, 512), BF16),
            pltpu.VMEM((64, 256), BF16),
            pltpu.VMEM((64, 256), BF16),
            pltpu.VMEM((2, 4, 64, 512), F32),
            pltpu.VMEM((2, 4, 64, 256), F32),
            dma((4,)),
            dma((4, 3)), dma((4, 3)),
            dma((4, 3)), dma((4, 3)),
            dma((4, 3)), dma((4, 3)),
            dma((4, 3)), dma((4, 3)),
            dma((4, 4, 3)), dma((4, 4, 3)),
            dma((4,)), dma((4,)),
            dma((2, 2, 3)), dma((2, 2, 3)),
            dma((2,)), dma((2,)),
        ],
        compiler_params=pltpu.CompilerParams(
            collective_id=0, has_side_effects=True, vmem_limit_bytes=56_000_000
        ),
    )(activations, left_factor, right_factor, out_grad)
    return pl.pallas_call(
        put_out,
        name="put_out",
        out_shape=tuple(jax.ShapeDtypeStruct(r.shape, r.dtype) for r in results),
        in_specs=[vmem] * 3,
        out_specs=(pl.BlockSpec(memory_space=pltpu.HBM),) * 3,
        scratch_shapes=[dma((3,))],
        compiler_params=pltpu.CompilerParams(vmem_limit_bytes=1024 * 1024),
    )(*results)


def solution(mesh):
    return jax.shard_map(
        shards,
        mesh=mesh,
        in_specs=(P("dp", "tensor"), P(None, "tensor"), P(None, "tensor"), P("dp", "tensor")),
        out_specs=(P("dp", "tensor"),) * 3,
        check_vma=False,
    )
```

```python
import functools
import math

import jax
import jax.numpy as jnp
from jax import lax
from jax.experimental import pallas as pl
from jax.experimental.pallas import tpu as pltpu
from jax.sharding import PartitionSpec as P

MESH = pl.DeviceIdType.MESH
F32, BF16 = jnp.float32, jnp.bfloat16
NT = (((1,), (1,)), ((), ()))
TN = (((0,), (0,)), ((), ()))
HALF = 256


def place(x, y, z, core):
    x, y, z, core = x % 4, y % 4, z % 16, core % 2
    return ((z % 8) * 2 + core, x * 8 + (z // 8) * 4 + y)


def kernel(
    scale,
    act_hbm, left_hbm, right_hbm, cot_hbm,
    ig_ref, lg_ref, rg_ref,
    act, left, right, cot,
    own1, snd1, rcv1, acc2, snd2, rcv2, acc3, snd3, rcv3, lat,
    latx, qs_r, qr_r, qs_l, qr_l, hs_r, hr_r, hs_l, hr_l, sum_r, sum_l,
    in_sem, s1, r1, s2, r2, s3, r3, s4, r4, s5, r5, sx, rx, sq, rq, sh, rh,
):
    d, t = lax.axis_index("dp"), lax.axis_index("tensor")
    x, y, core = t // 8, t % 4, d % 2
    zl = d // 2
    z = ((t // 4) % 2) * 8 + zl
    quad, pos = zl // 4, zl % 4
    outer = (pos == 0) | (pos == 3)
    inner = (pos == 1) | (pos == 2)
    near = pos + 1 - 2 * (pos % 2)
    cross, far = 3 - pos, 3 - near

    def coords(h):
        return (x, y) if h == 0 else (y, x)

    def along(h, da, db):
        return place(x + da, y + db, z, core) if h == 0 else place(x + db, y + da, z, core)

    def remote(src, dst, ssem, rsem, device):
        return pltpu.make_async_remote_copy(
            src_ref=src, dst_ref=dst, send_sem=ssem, recv_sem=rsem,
            device_id=device, device_id_type=MESH,
        )

    def mate(at):
        return place(x, y, z - pos + at, core)

    opposite = place(x, y, z + 4 - 8 * quad, core)

    loads = [
        pltpu.make_async_copy(src, dst, in_sem.at[i])
        for i, (src, dst) in enumerate(
            ((left_hbm, left), (act_hbm, act.at[core]), (right_hbm, right), (cot_hbm, cot.at[core]))
        )
    ]
    for load in loads:
        load.start()

    barrier = pltpu.get_barrier_semaphore()
    peers = [place(x, y, z + 8, core), place(x, y, z + 8, core + 1)]
    peers += [opposite, *(mate((pos + step) % 4) for step in (2, 1, 3))]
    peers += [place(x + k, y, z, core) for k in (2, 1, 3)] + [place(x, y + k, z, core) for k in (2, 1, 3)]
    peers += [place(x, y, z, core + 1)]
    for peer in peers:
        pl.semaphore_signal(barrier, inc=1, device_id=peer, device_id_type=MESH)

    def copy1(k, step):
        a, _ = coords(k % 2)
        return remote(
            snd1.at[k, (a + step) % 4], rcv1.at[k, step - 1], s1.at[k, step - 1], r1.at[k, step - 1],
            along(k % 2, step, 0),
        )

    def feature_copies():
        return [
            remote(src, dst.at[core], sx.at[i], rx.at[i], place(x, y, z, core + 1))
            for i, (src, dst) in enumerate(((cot_hbm, cot), (act_hbm, act)))
        ]

    def tiles(pair, weights, feats):
        tokens = pl.ds(pair % 2 * HALF, HALF)
        for h in range(2):
            k = pair * 2 + h
            rows = lax.dot_general(
                weights[h * 512 : h * 512 + 512, :], feats[core, tokens], NT, preferred_element_type=F32
            ).reshape(4, 2, 4, 16, HALF)
            for i in range(4):
                for c in range(2):
                    own1[k, i, :, c] = rows[i, c]
                    snd1[k, i, :, c] = rows[i, c].astype(BF16)

    def send1(pair, *steps):
        for step in steps:
            for h in range(2):
                copy1(pair * 2 + h, step).start()

    loads[0].wait()
    loads[1].wait()
    tiles(0, left, act)
    pl.semaphore_wait(barrier, len(peers))
    send1(0, 2, 1, 3)
    tiles(1, left, act)
    send1(1, 2)
    for copy in feature_copies():
        copy.start()
    loads[2].wait()
    loads[3].wait()
    tiles(2, right, cot)
    tiles(3, right, cot)

    def copy2(k, step):
        _, b = coords(k % 2)
        return remote(
            snd2.at[k, (b + step) % 4], rcv2.at[k, step - 1], s2.at[k, step - 1], r2.at[k, step - 1],
            along(k % 2, 0, step),
        )

    def second(k):
        for step in (1, 3, 2) if k >= 2 else (1, 3):
            copy1(k, step).wait_recv()
        a, _ = coords(k % 2)
        total = own1[k, a] + rcv1[k, 0].astype(F32) + rcv1[k, 1].astype(F32) + rcv1[k, 2].astype(F32)
        acc2[k] = total
        snd2[k] = total.astype(BF16)
        for step in (2, 1, 3):
            copy2(k, step).start()

    def copy3(k, way):
        source = snd3.at[k, core if way == 0 else 1 - core]
        device = (place(x, y, z + 8, core), place(x, y, z, core + 1), place(x, y, z + 8, core + 1))[way]
        return remote(source, rcv3.at[k, way], s3.at[k, way], r3.at[k, way], device)

    def third(k):
        _, b = coords(k % 2)
        for step in (1, 3, 2):
            copy2(k, step).wait_recv()
        total = acc2[k, b] + rcv2[k, 0].astype(F32) + rcv2[k, 1].astype(F32) + rcv2[k, 2].astype(F32)
        acc3[k] = total
        snd3[k] = total.astype(BF16)
        for way in (0, 2, 1):
            copy3(k, way).start()

    def copy4(k, step, arriving=False):
        a, b = coords(k % 2)
        block = lat.at[k, a, (b - step) % 4] if arriving else lat.at[k, a, b]
        return remote(block, block, s4.at[k, step - 1], r4.at[k, step - 1], along(k % 2, 0, step))

    def copy5(k, back, step, arriving=False):
        a, b = coords(k % 2)
        block = lat.at[k, (a - step) % 4 if arriving else a, (b - back) % 4]
        return remote(
            block, block, s5.at[k, back, step - 1], r5.at[k, back, step - 1], along(k % 2, step, 0)
        )

    def fourth(k):
        a, b = coords(k % 2)
        for way in (1, 0, 2):
            copy3(k, way).wait_recv()
        lat[k, a, b, core] = (acc3[k, core] + rcv3[k, 0].astype(F32)).astype(BF16)
        lat[k, a, b, 1 - core] = (rcv3[k, 1].astype(F32) + rcv3[k, 2].astype(F32)).astype(BF16)
        for step in (2, 1, 3):
            copy4(k, step).start()
        for step in (2, 1, 3):
            copy5(k, 0, step).start()

    def fifth(k):
        for back in (1, 3, 2):
            copy4(k, back, True).wait_recv()
            for step in (2, 1, 3):
                copy5(k, back, step).start()

    def gathered(k):
        for back in (0, 1, 3, 2):
            for step in (1, 3, 2):
                copy5(k, back, step, True).wait_recv()

    def both(stage, pair):
        for h in range(2):
            stage(pair * 2 + h)

    kinds = (
        (cot, qs_r, qr_r, hs_r, hr_r, sum_r, rg_ref),
        (act, qs_l, qr_l, hs_l, hr_l, sum_l, lg_ref),
    )

    def products(kind, part):
        feats, total = kinds[kind][0], kinds[kind][5]
        result = 0.0
        for u in range(2):
            k = kind * 4 + u * 2 + (quad if part else 1 - quad)
            for c in range(2):
                result += jnp.dot(
                    lat[k, :, :, c].reshape(256, HALF), feats[c, u * HALF : u * HALF + HALF],
                    preferred_element_type=F32,
                )
        total[part] = result.reshape(4, 64, feats.shape[2])

    def swap_copy(n):
        return remote(
            lat.at[4 + n, :, :, 1 - core], latx.at[n], sx.at[2 + n], rx.at[2 + n], place(x, y, z, core + 1)
        )

    def quad_copy(part, source, slot, at):
        qs, qr = kinds[0][1:3]
        return remote(
            qs.at[part, source], qr.at[part, slot],
            sq.at[0, part, source], rq.at[0, part, slot], mate(at),
        )

    def handed(part):
        return [quad_copy(part, n, n, near) for n in (2, 3)]

    def straight(part):
        return quad_copy(part, 0, 0, near)

    def passed(part):
        return [quad_copy(part, 2, 1, cross), quad_copy(part, 3, 1, far)]

    def quads(part):
        qs, total = kinds[0][1], kinds[0][5]
        qs[part, 0] = total[part, near].astype(BF16)

        @pl.when(outer)
        def _():
            qs[part, 2] = total[part, far].astype(BF16)
            qs[part, 3] = total[part, cross].astype(BF16)
            for copy in handed(part):
                copy.start()

        straight(part).start()

    def relays(part):
        qs, qr, total = kinds[0][1], kinds[0][2], kinds[0][5]

        @pl.when(inner)
        def _():
            for n, (copy, at) in enumerate(zip(handed(part), (cross, far))):
                copy.wait_recv()
                qs[part, 2 + n] = (total[part, at] + qr[part, 2 + n].astype(F32)).astype(BF16)
            for onward in passed(part):
                onward.start()

    def quad_sends(part):
        straight(part).wait_send()

        @pl.when(outer)
        def _():
            for copy in handed(part):
                copy.wait_send()

        @pl.when(inner)
        def _():
            for copy in passed(part):
                copy.wait_send()

    def run_sum(part):
        qr = kinds[0][2]
        total = kinds[0][5][part, pos]
        for slot in (0, 1):
            quad_copy(part, slot, slot, near).wait_recv()
            total = total + qr[part, slot].astype(F32)
        return total

    def direct_copy(part, step):
        return remote(
            qs_l.at[part, step - 1], qr_l.at[part, step - 1],
            sq.at[1, part, step - 1], rq.at[1, part, step - 1], mate((pos + step) % 4),
        )

    def direct(part):
        for step in (2, 1, 3):
            qs_l[part, step - 1] = sum_l[part, (pos + step) % 4].astype(BF16)
        for step in (2, 1, 3):
            direct_copy(part, step).start()

    def direct_sum(part):
        total = sum_l[part, pos]
        for step in (1, 3, 2):
            direct_copy(part, step).wait_recv()
            total = total + qr_l[part, step - 1].astype(F32)
        return total

    def half_copy(kind):
        hs, hr = kinds[kind][3:5]
        return remote(hs, hr, sh.at[kind], rh.at[kind], opposite)

    def halves(kind):
        hs = kinds[kind][3]
        hs[...] = (direct_sum(0) if kind else run_sum(0)).astype(BF16)
        half_copy(kind).start()

    def finish(kind):
        hr, out = kinds[kind][4], kinds[kind][6]
        total = direct_sum(1) if kind else run_sum(1)
        half_copy(kind).wait_recv()
        out[...] = (total + hr[...].astype(F32)) * scale

    send1(1, 1, 3)
    for h in range(2):
        copy1(h, 2).wait_recv()
    both(second, 0)
    send1(2, 2)
    both(second, 1)
    send1(2, 1, 3)
    both(third, 0)
    both(third, 1)
    send1(3, 2, 1, 3)
    both(second, 2)
    both(third, 2)
    both(second, 3)
    both(fourth, 0)
    both(third, 3)
    both(fourth, 1)
    both(fifth, 0)
    both(fifth, 1)
    for copy in feature_copies():
        copy.wait_recv()
    both(fourth, 2)
    both(gathered, 0)
    both(fourth, 3)
    both(gathered, 1)
    products(0, 0)
    quads(0)
    both(fifth, 2)
    both(fifth, 3)
    products(0, 1)
    quads(1)
    relays(0)
    both(gathered, 2)
    both(gathered, 3)
    products(1, 0)
    direct(0)
    relays(1)
    halves(0)
    products(1, 1)
    direct(1)
    for n in range(4):
        swap_copy(n).start()

    def ranks(h, c):
        return jnp.concatenate(
            [left[pl.ds(pl.multiple_of(h * 512 + i * 128 + c * 64, 64), 64), :] for i in range(4)], axis=0
        )

    halves(1)
    for n in range(4):
        swap_copy(n).wait_recv()
    for u in range(2):
        total = 0.0
        for h in range(2):
            n = u * 2 + h
            total += lax.dot_general(
                lat[4 + n, :, :, core].reshape(256, HALF), ranks(h, core), TN, preferred_element_type=F32
            )
            total += lax.dot_general(
                latx[n].reshape(256, HALF), ranks(h, 1 - core), TN, preferred_element_type=F32
            )
        ig_ref[u * HALF : u * HALF + HALF, :] = total.astype(BF16)
    finish(0)
    finish(1)

    for k in range(8):
        for step in (1, 2, 3):
            copy1(k, step).wait_send()
            copy2(k, step).wait_send()
            copy4(k, step).wait_send()
            for back in range(4):
                copy5(k, back, step).wait_send()
        for way in range(3):
            copy3(k, way).wait_send()
    for copy in feature_copies():
        copy.wait_send()
    for n in range(4):
        swap_copy(n).wait_send()
    for part in range(2):
        quad_sends(part)
        for step in (1, 2, 3):
            direct_copy(part, step).wait_send()
    for kind in range(2):
        half_copy(kind).wait_send()


def put_out(a, b, c, a_out, b_out, c_out, sem):
    copies = [
        pltpu.make_async_copy(src, dst, sem.at[i])
        for i, (src, dst) in enumerate(((a, a_out), (b, b_out), (c, c_out)))
    ]
    for copy in copies:
        copy.start()
    for copy in copies:
        copy.wait()


def shards(activations, left_factor, right_factor, out_grad):
    scale = 1.0 / math.sqrt(activations.shape[0] * lax.axis_size("dp"))
    hbm = pl.BlockSpec(memory_space=pltpu.HBM)
    vmem = pl.BlockSpec(memory_space=pltpu.VMEM)
    dma = pltpu.SemaphoreType.DMA
    results = pl.pallas_call(
        functools.partial(kernel, scale),
        name="lowrank_backward",
        out_shape=(
            jax.ShapeDtypeStruct((512, 256), BF16),
            jax.ShapeDtypeStruct((64, 256), F32),
            jax.ShapeDtypeStruct((64, 512), F32),
        ),
        in_specs=[hbm] * 4,
        out_specs=(vmem,) * 3,
        scratch_shapes=[
            pltpu.VMEM((2, 512, 256), BF16),
            pltpu.VMEM((1024, 256), BF16),
            pltpu.VMEM((1024, 512), BF16),
            pltpu.VMEM((2, 512, 512), BF16),
            pltpu.VMEM((8, 4, 4, 2, 16, 256), F32),
            pltpu.VMEM((8, 4, 4, 2, 16, 256), BF16),
            pltpu.VMEM((8, 3, 4, 2, 16, 256), BF16),
            pltpu.VMEM((8, 4, 2, 16, 256), F32),
            pltpu.VMEM((8, 4, 2, 16, 256), BF16),
            pltpu.VMEM((8, 3, 2, 16, 256), BF16),
            pltpu.VMEM((8, 2, 16, 256), F32),
            pltpu.VMEM((8, 2, 16, 256), BF16),
            pltpu.VMEM((8, 3, 16, 256), BF16),
            pltpu.VMEM((8, 4, 4, 2, 16, 256), BF16),
            pltpu.VMEM((4, 4, 4, 16, 256), BF16),
            pltpu.VMEM((2, 4, 64, 512), BF16),
            pltpu.VMEM((2, 4, 64, 512), BF16),
            pltpu.VMEM((2, 3, 64, 256), BF16),
            pltpu.VMEM((2, 3, 64, 256), BF16),
            pltpu.VMEM((64, 512), BF16),
            pltpu.VMEM((64, 512), BF16),
            pltpu.VMEM((64, 256), BF16),
            pltpu.VMEM((64, 256), BF16),
            pltpu.VMEM((2, 4, 64, 512), F32),
            pltpu.VMEM((2, 4, 64, 256), F32),
            dma((4,)),
            dma((8, 3)), dma((8, 3)),
            dma((8, 3)), dma((8, 3)),
            dma((8, 3)), dma((8, 3)),
            dma((8, 3)), dma((8, 3)),
            dma((8, 4, 3)), dma((8, 4, 3)),
            dma((6,)), dma((6,)),
            dma((2, 2, 4)), dma((2, 2, 4)),
            dma((2,)), dma((2,)),
        ],
        compiler_params=pltpu.CompilerParams(
            collective_id=0, has_side_effects=True, vmem_limit_bytes=56_000_000
        ),
    )(activations, left_factor, right_factor, out_grad)
    return pl.pallas_call(
        put_out,
        name="put_out",
        out_shape=tuple(jax.ShapeDtypeStruct(r.shape, r.dtype) for r in results),
        in_specs=[vmem] * 3,
        out_specs=(pl.BlockSpec(memory_space=pltpu.HBM),) * 3,
        scratch_shapes=[dma((3,))],
        compiler_params=pltpu.CompilerParams(vmem_limit_bytes=1024 * 1024),
    )(*results)


def solution(mesh):
    return jax.shard_map(
        shards,
        mesh=mesh,
        in_specs=(P("dp", "tensor"), P(None, "tensor"), P(None, "tensor"), P("dp", "tensor")),
        out_specs=(P("dp", "tensor"),) * 3,
        check_vma=False,
    )
```
